768 devices in a mesh: ctx: 32 (over y, x), exp: 12 (over z), tp: 2 (over core).
Axes of the slice: x: 4, y: 8, z: 12, core: 2. Of those that a mesh axis runs over, the one named last changes fastest.
Arguments:
- hidden: bfloat16 [49152, 4, 1408], P(('ctx', 'exp'), None, 'tp'), may hold values from -6 to 6
- expert_ids: int32 [49152, 4], P(('ctx', 'exp')), may hold values from 0 to 63, all different within a row; in each aligned block of 128 rows (0 to 127, 128 to 255, ...) at most 9 rows name the same one
- gate_fix: int32 [49152, 4], P(('ctx', 'exp')), may hold values from 1024 to 65535
- grad_out: bfloat16 [49152, 2048], P(('ctx', 'exp'), 'tp'), may hold values from -6 to 6
- w_down: bfloat16 [64, 1408, 2048], P('ctx', 'tp'), may hold values from -0.15625 to 0.15625
Outputs:
- mixed: bfloat16 [49152, 2048], P(('ctx', 'exp'), 'tp')
- grad_hidden: bfloat16 [49152, 4, 1408], P(('ctx', 'exp'), None, 'tp')
The draws below stay inside these ranges and needn't reach their ends.
Inputs may be any that keep to these rules, and one draw needn't show every extreme that they name: `expert_ids`: each row names 4 different experts. Within the 128 rows of one index of ctx and exp, no expert is named by more than 9 rows, a bound that some block reaches.
All inputs are finite; a program needn't handle non-finite values.
Results may differ from the reference program's by a relative error of at most 0.013.
Values may be sent and summed in bfloat16 or wider, within the bound.
A program may use at most 64 MiB of HBM per device.

```python
import math
import jax
import jax.numpy as jnp
import numpy as np
from jax import lax

D = 2048
FF = 1408
TOPK = 4
TOK_DEV = 128
EXPERTS = 64
CAP = 9
TOKENS = 49152
N_CTX = 32
N_EXP = 12
N_TP = 2


def plant(drawn, stream_key, smallest, largest):
    shape = drawn.shape
    spot = [jax.random.randint(jax.random.fold_in(stream_key, axis), (), 0, shape[axis]) for axis in range(len(shape))]
    drawn = drawn.at[tuple(spot)].set(smallest)
    longest = shape.index(max(shape))
    spot[longest] = (spot[longest] + 1) % shape[longest]
    return drawn.at[tuple(spot)].set(largest)


def block_scale(rng, shape, pieces, least, high):
    def one(axis_at, shards_of):
        draws = jax.random.uniform(jax.random.fold_in(jax.random.fold_in(rng, 6), axis_at), (shards_of,), jnp.float32, least / len(pieces), high / len(pieces))
        return jnp.repeat(jnp.exp(draws), shape[axis_at] // shards_of).reshape((-1,) + (1,) * (len(shape) - axis_at - 1))

    factor_of = one(*pieces[0])
    for cut in pieces[1:]:
        factor_of = factor_of * one(*cut)
    return factor_of


def shared_out(rng, own, number, rows, count, top, reach, skew):
    order = jax.random.permutation(rng, count)
    packed, common = load_shares(count, rows * top, reach, skew, True), load_shares(count, rows * top, reach, skew, False)
    places = jnp.arange(count)

    def named(tallies, turn):
        used = int((tallies > 0).sum())
        fixed = max(1, used // 4)
        shifted = fixed + (places - fixed + turn * (used - fixed)) % max(1, count - fixed)
        return jnp.zeros((count,), jnp.int32).at[order[jnp.where(places < fixed, places, shifted)]].set(jnp.asarray(tallies, jnp.int32))

    tallies = jnp.where(number % 4 == 0, named(packed, number // 4), named(common, number - number // 4 - 1))
    mixed = jax.random.permutation(jax.random.fold_in(own, 3), count)
    donor, sink = mixed[0:count // 2 * 2:2], mixed[1:count // 2 * 2:2]
    margin = jnp.minimum(tallies[donor] - 1, reach - tallies[sink]) // 2
    margin = jnp.where((donor == order[0]) | (sink == order[0]) | (tallies[sink] == 0), 0, jnp.maximum(margin, 0))
    shifted = jax.random.randint(jax.random.fold_in(own, 4), (count // 2,), 0, 1 << 20) % (margin + 1)
    tallies = tallies.at[donor].add(-shifted).at[sink].add(shifted)
    labels = jnp.searchsorted(jnp.cumsum(tallies), jnp.arange(rows * top), side="right").astype(jnp.int32)
    grid = labels.reshape(top, rows).T
    grid = grid[jax.random.permutation(jax.random.fold_in(own, 1), rows)]
    turn = jax.random.randint(jax.random.fold_in(own, 2), (rows, 1), 0, top)
    return jnp.take_along_axis(grid, (jnp.arange(top)[None, :] + turn) % top, axis=1)


def load_shares(amount, total, bound, lean, full):
    portions = [(1 << 20) // math.isqrt(grade ** lean) + 1 for grade in range(1, amount + 1)]
    largest = bound if full else min(bound, max(-(-total // amount), total * portions[0] // sum(portions)))
    least = 1 if total - largest >= amount - 1 else 0
    holding, spare = [largest] + [least] * (amount - 1), total - largest - least * (amount - 1)
    while spare > 0:
        movable = [i for i in range(1, amount) if holding[i] < largest] or [i for i in range(1, amount) if holding[i] < bound]
        whole, left = sum([portions[i] for i in movable]), spare
        for i in movable:
            addition = min(bound - holding[i], max(1, left * portions[i] // whole), spare)
            holding[i] = holding[i] + addition
            spare = spare - addition
    return np.array(holding)


def normal_values(stream_key, shape, scale, reach, shards=(), held_as=jnp.bfloat16):
    entries = scale * jax.random.normal(stream_key, shape, jnp.float32)
    if shards:
        entries = entries * block_scale(stream_key, shape, shards, -0.22, 0.18)
    return jnp.clip(entries, -reach, reach).astype(held_as)


def setup_inputs(seed: int = 0) -> dict:
    key_list = jax.random.split(jax.random.key(seed), 6)
    hidden = normal_values(key_list[0], (TOKENS, TOPK, FF), 1.0, 6.0, ((0, 384), (2, 2)))
    expert_ids_keys = jax.random.split(jax.random.fold_in(key_list[1], 1), TOKENS // TOK_DEV)
    expert_ids_turns = jax.random.permutation(jax.random.fold_in(key_list[1], 3), TOKENS // TOK_DEV)
    expert_ids = jax.vmap(lambda own, number: shared_out(jax.random.fold_in(key_list[1], 2), own, number, TOK_DEV, EXPERTS, TOPK, CAP, 2))(expert_ids_keys, expert_ids_turns).reshape((TOKENS, TOPK))
    gate_fix = plant(jax.random.randint(key_list[2], (TOKENS, TOPK), 1024, 65536), jax.random.fold_in(key_list[2], 1), 1024, 65535).astype(jnp.int32)
    grad_out = normal_values(key_list[3], (TOKENS, D), 1.0, 6.0, ((0, 384), (1, 2)))
    w_down = normal_values(key_list[4], (EXPERTS, FF, D), FF ** -0.5, 0.15625, ((0, 32), (1, 2)))
    return {"hidden": hidden, "expert_ids": expert_ids, "gate_fix": gate_fix, "grad_out": grad_out, "w_down": w_down}


def rounded_sum(partials):
    rounded = lax.optimization_barrier(partials.astype(jnp.bfloat16))
    return jnp.sum(rounded.astype(jnp.float32), axis=0)


def reference(hidden, expert_ids, gate_fix, grad_out, w_down):
    blocks = N_CTX * N_EXP
    per_block = TOK_DEV * TOPK
    block_width = FF // N_TP
    flat_ids = expert_ids.reshape(blocks, per_block)
    onehot = (flat_ids[:, :, None] == jnp.arange(EXPERTS, dtype=jnp.int32)[None, None, :]).astype(jnp.int32)
    before = jnp.cumsum(onehot, axis=1) - onehot
    position = jnp.sum(before * onehot, axis=2)
    target = (flat_ids * CAP + position).astype(jnp.int32)
    assign_index = jnp.arange(blocks * per_block, dtype=jnp.int32).reshape(blocks, per_block)
    block_index = jnp.arange(blocks, dtype=jnp.int32)[:, None]
    source = jnp.full((blocks, EXPERTS * CAP), blocks * per_block, jnp.int32).at[block_index, target].set(assign_index)
    source_by_expert = source.reshape(blocks, EXPERTS, CAP).transpose(1, 0, 2)
    gate_val = gate_fix.astype(jnp.float32) * (1.0 / 65536.0)
    gate_flat = gate_val.reshape(TOKENS * TOPK)
    hidden_flat = hidden.reshape(TOKENS * TOPK, FF)
    scaled = (gate_val[:, :, None] * grad_out[:, None, :].astype(jnp.float32)).astype(jnp.bfloat16)
    scaled = scaled.reshape(TOKENS * TOPK, D)

    def expert_step(carry, operands):
        mixed_sum, grad_rows = carry
        src, down_w = operands
        flat_src = src.reshape(blocks * CAP).astype(jnp.int32)
        h_rows = jnp.take(hidden_flat, flat_src, axis=0, mode="fill", fill_value=0)
        dy_rows = jnp.take(scaled, flat_src, axis=0, mode="fill", fill_value=0)
        gate_rows = jnp.take(gate_flat, flat_src, axis=0, mode="fill", fill_value=0)
        hid_blocks = h_rows.astype(jnp.float32).reshape(-1, N_TP, block_width)
        down_blocks = down_w.astype(jnp.float32).reshape(N_TP, block_width, D)
        part_y = jnp.einsum("rth,thd->trd", hid_blocks, down_blocks)
        y_rows = rounded_sum(part_y).astype(jnp.bfloat16)
        d_rows = jnp.dot(dy_rows, down_w.T, preferred_element_type=jnp.float32).astype(jnp.bfloat16)
        token_index = (flat_src // TOPK).astype(jnp.int32)
        mixed_sum = mixed_sum.at[token_index].add(gate_rows[:, None] * y_rows.astype(jnp.float32), mode="drop")
        grad_rows = grad_rows.at[flat_src].set(d_rows, mode="drop")
        return (mixed_sum, grad_rows), None

    start = (jnp.zeros((TOKENS, D), jnp.float32), jnp.zeros((TOKENS * TOPK, FF), jnp.bfloat16))
    (mixed_sum, grad_rows), unused = lax.scan(expert_step, start, (source_by_expert, w_down))
    return mixed_sum.astype(jnp.bfloat16), grad_rows.reshape(TOKENS, TOPK, FF)
```

```python
import jax
import jax.numpy as jnp
from jax import lax
from jax.experimental import pallas as pl
from jax.experimental.pallas import tpu as pltpu
from jax.sharding import PartitionSpec as P

MESH = pl.DeviceIdType.MESH
BF16 = jnp.bfloat16
F32 = jnp.float32

NX, NY = 4, 8
CHIPS = NX * NY
EXPERTS = 64
TOK = 128
TOPK = 4
DH = 1024
FH = 704
ROW = 1792
PIECE = 256
NPIECE = ROW // PIECE
COLS = ROW + PIECE
FAR = 12
SELF = 20


def dot(a, b, ca=1, cb=0):
    return lax.dot_general(a, b, (((ca,), (cb,)), ((), ())), preferred_element_type=F32)


def iota(shape, dim):
    return lax.broadcasted_iota(jnp.int32, shape, dim)


def onehot_bf16(mask):
    return jnp.where(mask, 1.0, 0.0).astype(BF16)


def fold(rows, groups, j):
    return onehot_bf16(iota((rows, groups), 0) == iota((rows, groups), 1) * 8 + j)


def unfold(groups, rows, j):
    return onehot_bf16(iota((groups, rows), 1) == iota((groups, rows), 0) * 8 + j)


def slots(ids_ref):
    upper = onehot_bf16(iota((TOK, TOK), 0) < iota((TOK, TOK), 1))
    carry = jnp.zeros((EXPERTS, 1), F32)
    out = []
    for k in range(TOPK):
        ids = ids_ref[k : k + 1, :]
        hot = jnp.where(iota((EXPERTS, TOK), 0) == ids, 1.0, 0.0)
        before = dot(hot.astype(BF16), upper) + carry
        pos = jnp.sum(hot * before, axis=0, keepdims=True).astype(jnp.int32)
        carry = carry + jnp.sum(hot, axis=1, keepdims=True)
        main = jnp.where(pos < 8, ids * 8 + pos, -1)
        last = jnp.where(pos == 8, ids, -1)
        out.append((main, last))
    return out


def pack_kernel(hid_ref, ids_ref, gate_ref, grad_ref, send_ref):
    where = slots(ids_ref)
    rows = EXPERTS * 8
    for last, count in ((False, rows), (True, EXPERTS)):
        hid = jnp.zeros((count, FH), F32)
        pick = jnp.zeros((count, TOK), F32)
        gates = jnp.zeros((count, TOK), F32)
        for k in range(TOPK):
            hit = iota((count, TOK), 0) == where[k][int(last)]
            gate = gate_ref[k : k + 1, :].astype(F32) * (1.0 / 65536.0)
            hot = jnp.where(hit, 1.0, 0.0)
            pick = pick + hot
            gates = gates + jnp.where(hit, gate, 0.0)
            hid = hid + dot(hot.astype(BF16), hid_ref[k], 1, 1)
        gate_col = jnp.sum(gates, axis=1, keepdims=True)
        dy = dot(pick.astype(BF16), grad_ref[...]) * gate_col
        if not last:
            send_ref[:, 0:DH] = dy.astype(BF16)
            send_ref[:, DH:ROW] = jnp.concatenate(
                [hid, jnp.zeros((count, ROW - DH - FH), F32)], axis=1
            ).astype(BF16)
        else:
            whole = jnp.concatenate(
                [dy, hid, jnp.zeros((count, ROW - DH - FH), F32)], axis=1
            ).astype(BF16)
            extra = jnp.zeros((rows, PIECE), F32)
            for j in range(NPIECE):
                extra = extra + dot(fold(rows, EXPERTS, j), whole[:, j * PIECE : (j + 1) * PIECE])
            send_ref[:, ROW:COLS] = extra.astype(BF16)


def combine_kernel(back_ref, ids_ref, gate_ref, mixed_ref, grad_hid_ref):
    where = slots(ids_ref)
    rows = EXPERTS * 8
    extra = back_ref[:, ROW:COLS]
    last_rows = jnp.concatenate(
        [dot(unfold(EXPERTS, rows, j), extra) for j in range(NPIECE)], axis=1
    ).astype(BF16)
    high = [jnp.zeros((n, TOK), F32) for n in (rows, EXPERTS)]
    low = [jnp.zeros((n, TOK), F32) for n in (rows, EXPERTS)]
    main_hid = back_ref[:, DH : DH + FH]
    last_hid = last_rows[:, DH : DH + FH]
    for k in range(TOPK):
        gate = gate_ref[k : k + 1, :]
        top = (gate // 256) * 256
        top_f = top.astype(F32) * (1.0 / 65536.0)
        bot_f = (gate - top).astype(F32) * (1.0 / 65536.0)
        hits = [iota((n, TOK), 0) == where[k][i] for i, n in enumerate((rows, EXPERTS))]
        for i in range(2):
            high[i] = high[i] + jnp.where(hits[i], top_f, 0.0)
            low[i] = low[i] + jnp.where(hits[i], bot_f, 0.0)
        grad_hid_ref[k] = (
            dot(main_hid, onehot_bf16(hits[0]), 0, 0) + dot(last_hid, onehot_bf16(hits[1]), 0, 0)
        ).astype(BF16)
    main_out = back_ref[:, 0:DH]
    last_out = last_rows[:, 0:DH]
    total = dot(high[0].astype(BF16), main_out, 0, 0) + dot(low[0].astype(BF16), main_out, 0, 0)
    total = total + dot(high[1].astype(BF16), last_out, 0, 0) + dot(low[1].astype(BF16), last_out, 0, 0)
    mixed_ref[...] = total.astype(BF16)


def exchange_kernel(
    send_ref, w_ref, back_ref, recv, ret, weights, lhs, last_res,
    w_send, w_recv, own_sem, go_send, go_recv, ret_send, ret_recv,
):
    me = lax.axis_index("ctx")
    core = lax.axis_index("tp")
    y, x = me // NX, lax.rem(me, NX)

    def chip(q, sign):
        dy = lax.rem(q // NX + 3, NY)
        dx = lax.rem(q, NX)
        return lax.rem(y + sign * dy + NY, NY) * NX + lax.rem(x + sign * dx + NX, NX)

    def others(lo, hi, body):
        if lo <= SELF < hi:
            lax.fori_loop(lo, SELF, lambda q, c: body(q), None)
            lax.fori_loop(SELF + 1, hi, lambda q, c: body(q), None)
        else:
            lax.fori_loop(lo, hi, lambda q, c: body(q), None)

    def rows(i):
        return pl.ds(pl.multiple_of(i * 8, 8), 8)

    barrier = pltpu.get_barrier_semaphore()

    def greet(q):
        for e in range(2):
            pl.semaphore_signal(
                barrier, inc=1, device_id={"ctx": chip(q, -1), "tp": e}, device_id_type=MESH
            )

    others(0, CHIPS, greet)
    pl.semaphore_signal(barrier, inc=1, device_id={"tp": 1 - core}, device_id_type=MESH)
    pl.semaphore_wait(barrier, 2 * CHIPS - 1)

    def go(q, e):
        d = chip(q, -1)
        return pltpu.make_async_remote_copy(
            src_ref=send_ref.at[rows(2 * d + e), :],
            dst_ref=recv.at[core, rows(q), :],
            send_sem=go_send.at[e, q],
            recv_sem=go_recv.at[core, q],
            device_id={"ctx": d, "tp": e},
            device_id_type=MESH,
        )

    def come(q, h):
        return pltpu.make_async_remote_copy(
            src_ref=send_ref.at[rows(0), :],
            dst_ref=recv.at[h, rows(q), :],
            send_sem=go_send.at[h, q],
            recv_sem=go_recv.at[h, q],
            device_id={"ctx": chip(q, 1), "tp": h},
            device_id_type=MESH,
        )

    def start_go(q):
        for e in range(2):
            go(q, e).start()

    others(0, FAR, start_go)
    w_copy = pltpu.make_async_remote_copy(
        src_ref=w_ref.at[1 - core],
        dst_ref=weights.at[core],
        send_sem=w_send,
        recv_sem=w_recv,
        device_id={"tp": 1 - core},
        device_id_type=MESH,
    )
    w_copy.start()
    w_own = pltpu.make_async_copy(w_ref.at[core], weights.at[core], own_sem.at[0])
    w_own.start()
    others(FAR, CHIPS, start_go)
    go(SELF, 1 - core).start()
    self_go = pltpu.make_async_copy(
        send_ref.at[rows(2 * me + core), :], recv.at[core, rows(SELF), :], own_sem.at[1]
    )
    self_go.start()

    def put(q, h):
        return pltpu.make_async_remote_copy(
            src_ref=ret.at[h, rows(q), :],
            dst_ref=back_ref.at[rows(2 * me + core), :],
            send_sem=ret_send.at[h, q],
            recv_sem=ret_recv.at[core, q],
            device_id={"ctx": chip(q, 1), "tp": h},
            device_id_type=MESH,
        )

    def got(q, e):
        return pltpu.make_async_remote_copy(
            src_ref=ret.at[e, rows(q), :],
            dst_ref=back_ref.at[rows(2 * chip(q, -1) + e), :],
            send_sem=ret_send.at[e, q],
            recv_sem=ret_recv.at[e, q],
            device_id={"ctx": chip(q, -1), "tp": e},
            device_id_type=MESH,
        )

    def compute(lo, hi):
        n = hi - lo
        main, pad = 8 * n, -(-n // 8) * 8
        total = main + pad
        first = lo * 8
        for h in range(2):
            lhs[h, 0:main, :] = recv[h, first : first + main, 0:ROW]
            extra = recv[h, first : first + main, ROW:COLS]
            for j in range(NPIECE):
                lhs[h, main:total, j * PIECE : (j + 1) * PIECE] = dot(
                    unfold(pad, main, j), extra
                ).astype(BF16)
        for b in range(4):
            h, at = b // 2, (b % 2) * 512
            cols = slice(b * 512, (b + 1) * 512)
            res = dot(lhs[0, 0:total, DH : DH + FH], weights[0, :, cols])
            res = (res + dot(lhs[1, 0:total, DH : DH + FH], weights[1, :, cols])).astype(BF16)
            ret[h, first : first + main, at : at + 512] = res[0:main]
            last_res[h, 0:pad, at : at + 512] = res[main:total]
        for h in range(2):
            res = dot(lhs[0, 0:total, 0:DH], weights[h, :, 0:DH], 1, 1)
            res = res + dot(lhs[1, 0:total, 0:DH], weights[h, :, DH : 2 * DH], 1, 1)
            res = jnp.concatenate([res, jnp.zeros((total, ROW - DH - FH), F32)], axis=1).astype(BF16)
            ret[h, first : first + main, DH:ROW] = res[0:main]
            last_res[h, 0:pad, DH:ROW] = res[main:total]
            extra = jnp.zeros((main, PIECE), F32)
            for j in range(NPIECE):
                extra = extra + dot(
                    fold(main, pad, j), last_res[h, 0:pad, j * PIECE : (j + 1) * PIECE]
                )
            ret[h, first : first + main, ROW:COLS] = extra.astype(BF16)

    def wait_come(q):
        for h in range(2):
            come(q, h).wait_recv()

    def start_put(q):
        for h in range(2):
            put(q, h).start()

    others(0, FAR, wait_come)
    w_own.wait()
    w_copy.wait_recv()
    compute(0, FAR)
    others(0, FAR, start_put)

    others(FAR, CHIPS, wait_come)
    come(SELF, 1 - core).wait_recv()
    self_go.wait()
    compute(FAR, CHIPS)
    others(FAR, CHIPS, start_put)
    put(SELF, 1 - core).start()
    self_put = pltpu.make_async_copy(
        ret.at[core, rows(SELF), :], back_ref.at[rows(2 * me + core), :], own_sem.at[2]
    )
    self_put.start()

    def drain(q):
        for e in range(2):
            go(q, e).wait_send()
            put(q, e).wait_send()
            got(q, e).wait_recv()

    others(0, CHIPS, drain)
    go(SELF, 1 - core).wait_send()
    put(SELF, 1 - core).wait_send()
    got(SELF, 1 - core).wait_recv()
    self_put.wait()
    w_copy.wait_send()


def vmem(n):
    return [pl.BlockSpec(memory_space=pltpu.VMEM)] * n


def body(hidden, expert_ids, gate_fix, grad_out, w_down):
    hid_t = jnp.transpose(hidden, (1, 2, 0))
    ids_t = jnp.transpose(expert_ids)
    gate_t = jnp.transpose(gate_fix)
    rows = EXPERTS * 8
    send = pl.pallas_call(
        pack_kernel,
        out_shape=jax.ShapeDtypeStruct((rows, COLS), BF16),
        in_specs=vmem(4),
        out_specs=vmem(1)[0],
        name="pack",
    )(hid_t, ids_t, gate_t, grad_out)
    back = pl.pallas_call(
        exchange_kernel,
        out_shape=jax.ShapeDtypeStruct((rows, COLS), BF16),
        in_specs=[vmem(1)[0], pl.BlockSpec(memory_space=pl.ANY)],
        out_specs=pl.BlockSpec(memory_space=pl.ANY),
        scratch_shapes=[
            pltpu.VMEM((2, CHIPS * 8, COLS), BF16),
            pltpu.VMEM((2, CHIPS * 8, COLS), BF16),
            pltpu.VMEM((2, FH, 2 * DH), BF16),
            pltpu.VMEM((2, 184, ROW), BF16),
            pltpu.VMEM((2, 24, ROW), BF16),
            pltpu.SemaphoreType.DMA,
            pltpu.SemaphoreType.DMA,
            pltpu.SemaphoreType.DMA((3,)),
            pltpu.SemaphoreType.DMA((2, CHIPS)),
            pltpu.SemaphoreType.DMA((2, CHIPS)),
            pltpu.SemaphoreType.DMA((2, CHIPS)),
            pltpu.SemaphoreType.DMA((2, CHIPS)),
        ],
        compiler_params=pltpu.CompilerParams(collective_id=0, has_side_effects=True),
        name="exchange",
    )(send, w_down)
    mixed, grad_t = pl.pallas_call(
        combine_kernel,
        out_shape=(
            jax.ShapeDtypeStruct((TOK, DH), BF16),
            jax.ShapeDtypeStruct((TOPK, FH, TOK), BF16),
        ),
        in_specs=vmem(3),
        out_specs=tuple(vmem(2)),
        name="combine",
    )(back, ids_t, gate_t)
    return mixed, jnp.transpose(grad_t, (2, 0, 1))


def solution(mesh):
    placed = (
        P(("ctx", "exp"), None, "tp"),
        P(("ctx", "exp"), None),
        P(("ctx", "exp"), None),
        P(("ctx", "exp"), "tp"),
        P("ctx", "tp", None),
    )
    return jax.shard_map(
        body,
        mesh=mesh,
        in_specs=placed,
        out_specs=(P(("ctx", "exp"), "tp"), P(("ctx", "exp"), None, "tp")),
        check_vma=False,
    )
```
